512 devices in a mesh: lon: 16 (over z_hi, x, core), lat: 32 (over z_lo, y).
Axes of the slice: x: 4, y: 8, z: 8 (z_hi: 2, z_lo: 4; z = z_hi * 4 + z_lo), core: 2. Of those that a mesh axis runs over, the one named last changes fastest.
Arguments:
- model_state: float32 [4, 8, 1024, 5760], P(None, None, 'lat', 'lon')
- courant: float32 [1024], P('lat'), may hold values from 0.02 to 0.08
- cutoff: int32 [1024], replicated, may hold values from 1 to 2880, as said below
Outputs:
- new_state: float32 [4, 8, 1024, 5760], P(None, None, 'lat', 'lon')
The draws below stay inside these ranges and needn't reach their ends.
Inputs may be any that keep to these rules, and one draw needn't show every extreme that they name: `cutoff`: rows 256 to 767 hold 5760/2 (no damping); every other row holds less.
All inputs are finite; a program needn't handle non-finite values.
Results may differ from the reference program's by a relative error of at most 0.000073.
Values sent between devices are 32-bit elements; how exact they have to be, the bound alone decides.
No kernel may reach another device: no remote copies, remote signals or barrier semaphores. Data moves between devices by JAX's collectives and lax.ppermute only.
A program may use at most 64 MiB of HBM per device.

```python
import math
import jax
import jax.numpy as jnp
from jax import lax

NLON = 5760
LEV = 8
NLAT = 1024


def draw_model_state(key, part):
    key_list = jax.random.split(jax.random.fold_in(key, 11), 4)
    field_shape = (LEV, NLAT, NLON)
    wind_east = jax.random.truncated_normal(key_list[0], -3.0, 3.0, field_shape, jnp.float32)
    wind_north = jax.random.truncated_normal(key_list[1], -3.0, 3.0, field_shape, jnp.float32)
    theta = jnp.exp(jax.random.uniform(key_list[2], field_shape, jnp.float32, math.log(0.5), math.log(2.0)))
    thickness = jax.random.uniform(key_list[3], field_shape, jnp.float32, 2.0, 3.0)
    return jnp.stack([wind_east, wind_north, theta, thickness]).astype(jnp.float32)


def draw_cutoff(key, part):
    row_index = jnp.arange(NLAT, dtype=jnp.int32)
    quarter = NLAT // 4
    distance = jnp.where(row_index < quarter, row_index, NLAT - 1 - row_index)
    base_cut = NLON // 2 * (2 * distance + 1) // (2 * quarter)
    jitter = jax.random.randint(jax.random.fold_in(key, 23), (NLAT,), 0, 1048576) % (base_cut // 4 + 1)
    polar_cut = jnp.maximum(1, base_cut - jitter)
    is_polar = (row_index < quarter) | (row_index >= NLAT - quarter)
    return jnp.where(is_polar, polar_cut, NLON // 2).astype(jnp.int32)


def shard_levels(key, extent, shards, low, largest):
    factor_of, own = 1.0, jax.random.fold_in(key, 6)
    for position, parts in shards:
        draws = jnp.exp(jax.random.uniform(jax.random.fold_in(own, position), (parts,), jnp.float32, low / len(shards), largest / len(shards)))
        factor_of = factor_of * jnp.repeat(draws, extent[position] // parts).reshape([-1 if axis == position else 1 for axis in range(len(extent))])
    return factor_of


def setup_inputs(seed: int = 0) -> dict:
    arg_keys = jax.random.split(jax.random.key(seed), 4)
    return {
        "model_state": draw_model_state(jax.random.fold_in(arg_keys[3], 71), 0),
        "courant": jnp.clip(jnp.exp(math.log(0.08) - 1.3862944 * jax.random.uniform(arg_keys[1], (NLAT,), jnp.float32) ** shard_levels(arg_keys[1], (NLAT,), ((0, 32),), -0.2, 0.2)), 0.02, 0.08),
        "cutoff": draw_cutoff(jax.random.fold_in(arg_keys[3], 71), 0),
    }


meridional_courant = 0.05
pressure_gain = 4.0


def along_lon(field):
    return (jnp.roll(field, -1, axis=-1) - jnp.roll(field, 1, axis=-1)) * 0.5


def along_lat(field):
    padded = jnp.pad(field, ((0, 0), (1, 1), (0, 0)))
    return (padded[:, 2:, :] - padded[:, :-2, :]) * 0.5


def reference(model_state, courant, cutoff):
    wind_east = model_state[0]
    wind_north = model_state[1]
    theta = model_state[2]
    thickness = model_state[3]
    row_courant = courant[None, :, None]
    east_flux = wind_east * thickness
    north_flux = wind_north * thickness
    new_thickness = thickness - row_courant * along_lon(east_flux) - meridional_courant * along_lat(north_flux)
    heat_content = theta * thickness
    new_heat = heat_content - row_courant * along_lon(east_flux * theta) - meridional_courant * along_lat(north_flux * theta)
    new_theta = new_heat / new_thickness
    new_east = wind_east - pressure_gain * row_courant * along_lon(new_heat)
    new_north = wind_north - pressure_gain * meridional_courant * along_lat(new_heat)
    stacked = jnp.stack([new_east, new_north, new_theta, new_thickness])
    wave_number = jnp.arange(NLON, dtype=jnp.int32)
    folded = jnp.minimum(wave_number, NLON - wave_number)
    cut_ratio = cutoff.astype(jnp.float32)[:, None] / jnp.maximum(folded, 1).astype(jnp.float32)[None, :]
    damping = jnp.minimum(1.0, cut_ratio * cut_ratio)

    def filter_field(field):
        spectrum = jnp.fft.fft(field, axis=-1)
        return jnp.real(jnp.fft.ifft(spectrum * damping[None], axis=-1))

    filtered = lax.map(filter_field, stacked)
    return filtered.astype(jnp.float32)
```

```python
import math

import jax
import jax.numpy as jnp
import numpy as np
from jax import lax
from jax.experimental import pallas as pl
from jax.experimental.pallas import tpu as pltpu
from jax.sharding import PartitionSpec as P

slabs = 16
width = 360
circle = slabs * width
lanes = 384
fields = 4
half_rows = 16
lines = fields * half_rows
halo_lines = 8
freqs = slabs // 2 + 1

cross = 0.05 * 0.5
push_north = 4.0 * 0.05 * 0.5
push_east = 4.0 * 0.5


def width_tables():
    r = np.arange(width)
    angle = 2.0 * np.pi * ((r[:, None] * r[None, :]) % width) / width
    cos, sin = np.cos(angle), np.sin(angle)
    table = np.zeros((2 * lanes, 2 * lanes), np.float64)
    table[:width, :width] = cos
    table[:width, lanes : lanes + width] = -sin
    table[lanes : lanes + width, :width] = sin
    table[lanes : lanes + width, lanes : lanes + width] = cos
    high = table.astype(jnp.bfloat16)
    low = (table - high.astype(np.float64)).astype(jnp.bfloat16)
    return high, low


def line_tables():
    r = np.arange(width)
    twist = np.zeros((2, slabs, lanes), np.float32)
    inverse = np.zeros((freqs, 1, 2 * lanes), np.float32)
    for k in range(freqs):
        angle = 2.0 * np.pi * (k * r) / circle
        twist[0, k, :width] = np.cos(angle)
        twist[1, k, :width] = np.sin(angle)
        wave = k + slabs * r
        folded = np.maximum(np.minimum(wave, circle - wave), 1)
        inverse[k, 0, :width] = 1.0 / folded
        inverse[k, 0, lanes : lanes + width] = 1.0 / folded
    return twist, inverse


def real_forward(x):
    n = len(x)
    if n == 1:
        return [(x[0], None)]
    if n == 2:
        return [(x[0] + x[1], None), (x[0] - x[1], None)]
    even, odd = real_forward(x[0::2]), real_forward(x[1::2])
    out = [None] * (n // 2 + 1)
    out[0] = (even[0][0] + odd[0][0], None)
    out[n // 2] = (even[0][0] - odd[0][0], None)
    out[n // 4] = (even[n // 4][0], -odd[n // 4][0])
    for k in range(1, n // 4):
        c, s = math.cos(2 * math.pi * k / n), math.sin(2 * math.pi * k / n)
        (er, ei), (qr, qi) = even[k], odd[k]
        if 8 * k == n:
            tr, ti = (qr + qi) * c, (qi - qr) * c
        else:
            tr, ti = qr * c + qi * s, qi * c - qr * s
        out[k] = (er + tr, ei + ti)
        out[n // 2 - k] = (er - tr, ti - ei)
    return out


def real_inverse(bins):
    n = 2 * (len(bins) - 1)
    if n == 2:
        return [bins[0][0] + bins[1][0], bins[0][0] - bins[1][0]]
    even, odd = [None] * (n // 4 + 1), [None] * (n // 4 + 1)
    even[0] = (bins[0][0] + bins[n // 2][0], None)
    odd[0] = (bins[0][0] - bins[n // 2][0], None)
    mid = bins[n // 4]
    even[n // 4] = (mid[0] + mid[0], None)
    odd[n // 4] = (-(mid[1] + mid[1]), None)
    for k in range(1, n // 4):
        c, s = math.cos(2 * math.pi * k / n), math.sin(2 * math.pi * k / n)
        (ar, ai), (br, bi) = bins[k], bins[n // 2 - k]
        even[k] = (ar + br, ai - bi)
        dr, di = ar - br, ai + bi
        if 8 * k == n:
            odd[k] = ((dr - di) * c, (di + dr) * c)
        else:
            odd[k] = (dr * c - di * s, di * c + dr * s)
    evens, odds = real_inverse(even), real_inverse(odd)
    out = [None] * n
    out[0::2], out[1::2] = evens, odds
    return out


def circle_kernel(
    raw, courant, cutoff, rim, twist, inverse, high, low, out, flux_a, flux_b, heat, heat_rim, work, part_high, part_low, spectrum
):
    lane = lax.broadcasted_iota(jnp.int32, (half_rows, lanes), 1)
    row = lax.broadcasted_iota(jnp.int32, (half_rows, lanes), 0)
    valid = lane < width

    def after(value, follower):
        return jnp.where(lane[: value.shape[0]] == width - 1, follower, pltpu.roll(value, lanes - 1, 1))

    def before(value, leader):
        return jnp.where(lane[: value.shape[0]] == 0, leader, pltpu.roll(value, 1, 1))

    def sides(s):
        return lax.rem(s + 1, slabs), lax.rem(s + slabs - 1, slabs)

    def north_minus_south(value, top, bottom):
        ahead = jnp.where(row == half_rows - 1, bottom, pltpu.roll(value, half_rows - 1, 0))
        behind = jnp.where(row == 0, top, pltpu.roll(value, 1, 0))
        return ahead - behind

    def east_minus_west(ref, s):
        ahead, behind = sides(s)
        value = ref[s]
        return after(value, ref[ahead, :, 0:1]) - before(value, ref[behind, :, width - 1 : width])

    def products(s, carry):
        flux = raw[s, 0:16, :] * raw[s, 48:64, :]
        flux_a[s] = flux
        flux_b[s] = flux * raw[s, 32:48, :]
        return carry

    lax.fori_loop(0, slabs, products, 0)

    def advance(s, carry):
        theta, thick = raw[s, 32:48, :], raw[s, 48:64, :]
        north = raw[s, 16:32, :] * thick
        north_heat = north * theta
        pace = courant[...] * 0.5
        new_thick = (
            thick
            - pace * east_minus_west(flux_a, s)
            - cross * north_minus_south(north, raw[s, 70:71, :], raw[s, 71:72, :])
        )
        new_heat = (
            theta * thick
            - pace * east_minus_west(flux_b, s)
            - cross * north_minus_south(north_heat, raw[s, 68:69, :], raw[s, 69:70, :])
        )
        heat[s] = new_heat
        work[s, 48:64, :] = jnp.where(valid, new_thick, 0.0)
        work[s, 32:48, :] = jnp.where(valid, new_heat / new_thick, 0.0)
        ahead, behind = sides(s)
        slope = after(raw[s, 66:68, :], raw[ahead, 66:68, 0:1]) - before(
            raw[s, 66:68, :], raw[behind, 66:68, width - 1 : width]
        )
        inner = jnp.concatenate([-north_heat[0:1], north_heat[half_rows - 1 : half_rows]], axis=0)
        heat_rim[s] = (raw[s, 64:66, :] - 0.5 * slope + cross * inner) * rim[...]
        return carry

    lax.fori_loop(0, slabs, advance, 0)

    def push(s, carry):
        new_east = raw[s, 0:16, :] - (push_east * courant[...]) * east_minus_west(heat, s)
        new_north = raw[s, 16:32, :] - push_north * north_minus_south(heat[s], heat_rim[s, 0:1, :], heat_rim[s, 1:2, :])
        work[s, 0:16, :] = jnp.where(valid, new_east, 0.0)
        work[s, 16:32, :] = jnp.where(valid, new_north, 0.0)
        return carry

    lax.fori_loop(0, slabs, push, 0)

    def split_into(rows, columns, value):
        upper = value.astype(jnp.bfloat16)
        part_high[rows, columns] = upper
        part_low[rows, columns] = (value - upper.astype(jnp.float32)).astype(jnp.bfloat16)

    def across(f, carry):
        for tile in range(lanes // 128):
            here = slice(tile * 128, tile * 128 + 128)
            there = slice(lanes + tile * 128, lanes + tile * 128 + 128)
            bins = real_forward([work[s, pl.ds(f * half_rows, half_rows), here] for s in range(slabs)])
            for k, (re, im) in enumerate(bins):
                rows = pl.ds(k * lines + f * half_rows, half_rows)
                if k == 0:
                    split_into(rows, here, re)
                    split_into(rows, there, jnp.zeros_like(re))
                    continue
                cos, sin = twist[0, k : k + 1, here], twist[1, k : k + 1, here]
                if im is None:
                    split_into(rows, here, re * cos)
                    split_into(rows, there, -(re * sin))
                else:
                    split_into(rows, here, re * cos + im * sin)
                    split_into(rows, there, im * cos - re * sin)
        return carry

    lax.fori_loop(0, fields, across, 0)

    def along(n, carry):
        columns = pl.ds(pl.multiple_of(n * 256, 256), 256)
        table = high[:, columns]
        total = jnp.dot(part_high[...], table, preferred_element_type=jnp.float32)
        total += jnp.dot(part_low[...], table, preferred_element_type=jnp.float32)
        total += jnp.dot(part_high[...], low[:, columns], preferred_element_type=jnp.float32)
        spectrum[:, columns] = total
        return carry

    lax.fori_loop(0, 2 * lanes // 256, along, 0)

    def damp(k, carry):
        for tile in range(2 * lanes // 128):
            here = slice(tile * 128, tile * 128 + 128)
            target = (tile + lanes // 128) % (2 * lanes // 128)
            there = slice(target * 128, target * 128 + 128)
            ratio = cutoff[...] * inverse[k, :, here]
            factor = jnp.minimum(1.0, ratio * ratio) * (1.0 / circle)
            for f in range(fields):
                rows = pl.ds(pl.multiple_of(k * lines + f * half_rows, half_rows), half_rows)
                split_into(rows, there, spectrum[rows, here] * factor)
        return carry

    lax.fori_loop(0, freqs, damp, 0)
    lax.fori_loop(0, 2 * lanes // 256, along, 0)

    def back(f, carry):
        for tile in range(lanes // 128):
            here = slice(tile * 128, tile * 128 + 128)
            there = slice(lanes + tile * 128, lanes + tile * 128 + 128)
            bins = []
            for k in range(freqs):
                rows = pl.ds(pl.multiple_of(k * lines + f * half_rows, half_rows), half_rows)
                re = spectrum[rows, there]
                if k == 0:
                    bins.append((re, None))
                    continue
                im = spectrum[rows, here]
                cos, sin = twist[0, k : k + 1, here], twist[1, k : k + 1, here]
                turned = re * cos - im * sin
                bins.append((turned, None if k == freqs - 1 else im * cos + re * sin))
            for s, value in enumerate(real_inverse(bins)):
                out[s, pl.ds(f * half_rows, half_rows), here] = value
        return carry

    lax.fori_loop(0, fields, back, 0)


def filter_circles(raw, courant, cutoff, rim):
    twist, inverse = line_tables()
    high, low = width_tables()
    scratch = [
        pltpu.VMEM((slabs, half_rows, lanes), jnp.float32),
        pltpu.VMEM((slabs, half_rows, lanes), jnp.float32),
        pltpu.VMEM((slabs, half_rows, lanes), jnp.float32),
        pltpu.VMEM((slabs, 2, lanes), jnp.float32),
        pltpu.VMEM((slabs, lines, lanes), jnp.float32),
        pltpu.VMEM((freqs * lines, 2 * lanes), jnp.bfloat16),
        pltpu.VMEM((freqs * lines, 2 * lanes), jnp.bfloat16),
        pltpu.VMEM((freqs * lines, 2 * lanes), jnp.float32),
    ]
    return pl.pallas_call(
        circle_kernel,
        out_shape=jax.ShapeDtypeStruct((slabs, lines, lanes), jnp.float32),
        in_specs=[pl.BlockSpec(memory_space=pltpu.VMEM)] * 8,
        out_specs=pl.BlockSpec(memory_space=pltpu.VMEM),
        scratch_shapes=scratch,
        compiler_params=pltpu.CompilerParams(vmem_limit_bytes=40 << 20),
        name="circles",
    )(raw, courant, cutoff, rim, jnp.asarray(twist), jnp.asarray(inverse), jnp.asarray(high), jnp.asarray(low))


def rim_terms(block, courant, row, inner):
    east, north, theta, thick = (block[i, :, row] for i in range(4))
    heat = theta * thick
    north_flux = north * thick
    sign = 1.0 if inner < row else -1.0
    outer = block[1, :, inner] * block[3, :, inner] * block[2, :, inner]
    return jnp.stack([heat + sign * cross * outer, courant[row] * (east * heat), north_flux * theta, north_flux])


def on_circles(block, courant, cutoff, top, bottom):
    levels, rows_here = block.shape[1:3]
    count = lax.axis_size("lat")
    band = lax.axis_index("lat")
    half = lax.axis_index("lon") % 2
    main = block.reshape(fields, levels, 2, half_rows, width).transpose(1, 2, 0, 3, 4).reshape(slabs, lines, width)
    tops = jnp.stack([top, rim_terms(block, courant, half_rows - 1, half_rows - 2)], axis=2)
    bottoms = jnp.stack([rim_terms(block, courant, half_rows, half_rows + 1), bottom], axis=2)
    rims = jnp.stack([tops, bottoms], axis=3).transpose(1, 2, 0, 3, 4).reshape(slabs, halo_lines, width)
    sent = jnp.pad(jnp.concatenate([main, rims], axis=1), ((0, 0), (0, 0), (0, lanes - width)))
    raw = lax.all_to_all(sent, "lon", 0, 0, tiled=True)
    own_courant = lax.dynamic_slice_in_dim(courant, half * half_rows, half_rows)
    own_cutoff = lax.dynamic_slice_in_dim(cutoff, band * rows_here + half * half_rows, half_rows).astype(jnp.float32)
    inside = jnp.stack([jnp.logical_or(band > 0, half > 0), jnp.logical_or(band < count - 1, half < 1)])
    smooth = filter_circles(
        raw,
        jnp.broadcast_to(own_courant[:, None], (half_rows, lanes)),
        jnp.broadcast_to(own_cutoff[:, None], (half_rows, 128)),
        jnp.broadcast_to(inside.astype(jnp.float32)[:, None], (2, lanes)),
    )
    returned = lax.all_to_all(smooth, "lon", 0, 0, tiled=True)
    returned = returned.reshape(levels, 2, fields, half_rows, lanes).transpose(2, 0, 1, 3, 4)
    return returned.reshape(fields, levels, rows_here, lanes)[..., :width]


def east_minus_west(value):
    return value[..., 2:] - value[..., :-2]


def north_minus_south(value, top, bottom):
    extended = jnp.concatenate([top[:, None], value, bottom[:, None]], axis=1)
    return extended[:, 2:] - extended[:, :-2]


def on_blocks(block, courant, cutoff, top, bottom):
    del cutoff
    levels, rows_here, width_here = block.shape[1:]
    count = lax.axis_size("lon")
    wind_east, wind_north, theta, thick = block[0], block[1], block[2], block[3]
    pace = courant[None, :, None] * 0.5
    east = wind_east * thick
    east_heat = east * theta
    north = wind_north * thick
    north_heat = north * theta
    heat = theta * thick - cross * north_minus_south(north_heat, top[2], bottom[2])
    slow = thick - cross * north_minus_south(north, top[3], bottom[3])

    def edge(at, inner, sign):
        pieces = [heat[..., at] + sign * pace[..., 0] * east_heat[..., inner], east_heat[..., at], east[..., at]]
        flat = [p.reshape(-1) for p in pieces] + [top[1][:, at], bottom[1][:, at]]
        return jnp.concatenate(flat)

    onward = [(i, (i + 1) % count) for i in range(count)]
    backward = [(j, i) for i, j in onward]
    west = lax.ppermute(edge(width_here - 1, width_here - 2, 1.0), "lon", onward)
    east_side = lax.ppermute(edge(0, 1, -1.0), "lon", backward)
    plane = levels * rows_here

    def opened(flat):
        three = flat[: 3 * plane].reshape(3, levels, rows_here, 1)
        two = flat[3 * plane :].reshape(2, levels, 1)
        return three, two

    (west_heat, west_east_heat, west_east), west_rims = opened(west)
    (east_heat_side, east_east_heat, east_east), east_rims = opened(east_side)
    wide = jnp.concatenate([west_east, east, east_east], axis=-1)
    wide_heat = jnp.concatenate([west_east_heat, east_heat, east_east_heat], axis=-1)
    new_thick = slow - pace * east_minus_west(wide)
    new_heat = heat - pace * east_minus_west(wide_heat)
    beyond_west = west_heat - pace * east_heat[..., :1]
    beyond_east = east_heat_side + pace * east_heat[..., -1:]
    top_flux = jnp.concatenate([west_rims[0], top[1], east_rims[0]], axis=-1)
    bottom_flux = jnp.concatenate([west_rims[1], bottom[1], east_rims[1]], axis=-1)
    top_heat = top[0] - 0.5 * east_minus_west(top_flux) - cross * north_heat[:, 0]
    bottom_heat = bottom[0] - 0.5 * east_minus_west(bottom_flux) + cross * north_heat[:, -1]
    new_east = wind_east - 4.0 * pace * east_minus_west(jnp.concatenate([beyond_west, new_heat, beyond_east], axis=-1))
    new_north = wind_north - push_north * north_minus_south(new_heat, top_heat, bottom_heat)
    return jnp.stack([new_east, new_north, new_heat / new_thick, new_thick])


def per_device(model_state, courant, cutoff):
    rows_here = model_state.shape[2]
    count = lax.axis_size("lat")
    band = lax.axis_index("lat")
    up = [(i, i + 1) for i in range(count - 1)]
    down = [(i + 1, i) for i in range(count - 1)]
    top = lax.ppermute(rim_terms(model_state, courant, rows_here - 1, rows_here - 2), "lat", up)
    bottom = lax.ppermute(rim_terms(model_state, courant, 0, 1), "lat", down)
    polar = jnp.logical_or(4 * band < count, 4 * band >= 3 * count)
    return lax.cond(polar, on_circles, on_blocks, model_state, courant, cutoff, top, bottom)


def solution(mesh):
    placed = (P(None, None, "lat", "lon"), P("lat"), P())
    return jax.shard_map(
        per_device,
        mesh=mesh,
        in_specs=placed,
        out_specs=P(None, None, "lat", "lon"),
        check_vma=False,
    )
```
